32 devices in a mesh: groups: 2 (over y), sample: 2 (over core), space: 8 (over z, x).
Axes of the slice: x: 2, y: 2, z: 4, core: 2. Of those that a mesh axis runs over, the one named last changes fastest.
Arguments:
- features: bfloat16 [4, 16, 16, 16, 128], P(('groups', 'sample'), 'space'), parts along dimension 0, may hold values from -6 to 6
- w_fine: bfloat16 [27, 128, 128], replicated, may hold values from -0.109375 to 0.109375
- w_down: bfloat16 [8, 128, 256], replicated, may hold values from -0.1875 to 0.1875
- mixing: bfloat16 [8, 8], replicated, may hold values from -2 to 2
- cotangent: bfloat16 [4, 8, 16384], P(('groups', 'sample'), None, 'space'), parts along dimension 0, may hold values from -6 to 6
Outputs:
- bottleneck: bfloat16 [4, 8, 16384], P(('groups', 'sample'), None, 'space'), parts along dimension 0
- feature_grad: bfloat16 [4, 16, 16, 16, 128], P(('groups', 'sample'), 'space'), parts along dimension 0
- fine_grad: float32 [884736], P(('groups', 'space')), parts along dimension 0
- down_grad: float32 [524288], P(('groups', 'space')), parts along dimension 0
- mixing_grad: float32 [16, 8], P(('groups', 'space')), parts along dimension 0
The draws below stay inside these ranges and needn't reach their ends.
There are 2 independent parts, one for each index of `groups`. The reference program is written for one: setup_inputs(seed, part) draws one part's arguments, and reference() takes and returns one part's arrays. A program takes and returns all parts, laid end to end along the dimension named above; an argument that names none is the same for every part. Nothing has to cross between parts.
All inputs are finite; a program needn't handle non-finite values.
Results may differ from the reference program's by a relative error of at most 0.0065.
Values may be sent and summed in bfloat16 or wider, within the bound.
A program may use at most 64 MiB of HBM per device.

```python
import jax
import jax.numpy as jnp
from jax import lax

C1 = 128
C2 = 256
WX = 16
WZ = 16
BATCH = 2
NY = 16
NYC = 8
PLANE = 64


def block_scale(own_key, dims, split, least, top_value):
    loudness, own = 1.0, jax.random.fold_in(own_key, 6)
    for dim, parts in split:
        draws = jnp.exp(jax.random.uniform(jax.random.fold_in(own, dim), (parts,), jnp.float32, least / len(split), top_value / len(split)))
        loudness = loudness * jnp.repeat(draws, dims[dim] // parts).reshape([-1 if axis == dim else 1 for axis in range(len(dims))])
    return loudness


def normal_values(rng, extent, scale, limit, cuts=(), kind=jnp.bfloat16):
    array = scale * jax.random.normal(rng, extent, jnp.float32)
    if cuts:
        array = array * block_scale(rng, extent, cuts, -0.22, 0.18)
    return jnp.clip(array, -limit, limit).astype(kind)


def setup_inputs(seed: int = 0, part: int = 0) -> dict:
    seeds = jax.random.split(jax.random.key(seed), 6)
    part_splits = jax.random.split(jax.random.fold_in(seeds[5], part), 6)
    features = normal_values(part_splits[0], (BATCH, NY, WX, WZ, C1), 1.0, 6.0, ((0, 2), (1, 8)))
    w_fine = normal_values(seeds[1], (27, C1, C1), (27 * C1) ** -0.5, 0.109375)
    w_down = normal_values(seeds[2], (8, C1, C2), (8 * C1) ** -0.5, 0.1875)
    mixing = normal_values(seeds[3], (NYC, NYC), NYC ** -0.5, 2.0)
    cotangent = normal_values(part_splits[4], (BATCH, NYC, PLANE * C2), 1.0, 6.0, ((0, 2), (2, 8)))
    return {"features": features, "w_fine": w_fine, "w_down": w_down, "mixing": mixing, "cotangent": cotangent}


def forward_conv(padded, weight, count):
    extent_x = padded.shape[2] - 2
    extent_z = padded.shape[3] - 2
    channels = padded.shape[4]
    total = None
    for shift_y in range(3):
        for shift_x in range(3):
            pieces = [padded[:, shift_y:shift_y + count, shift_x:shift_x + extent_x, shift_z:shift_z + extent_z, :] for shift_z in range(3)]
            stacked = jnp.concatenate(pieces, axis=-1).reshape(-1, 3 * channels)
            first = shift_y * 9 + shift_x * 3
            kernel = weight[first:first + 3].reshape(3 * channels, weight.shape[2])
            term = jnp.dot(stacked, kernel, preferred_element_type=jnp.float32)
            total = term if total is None else total + term
    return total.reshape(padded.shape[0], count, extent_x, extent_z, weight.shape[2])


def transposed_conv(padded, weight, count):
    extent_x = padded.shape[2] - 2
    extent_z = padded.shape[3] - 2
    channels = padded.shape[4]
    total = None
    for shift_y in range(3):
        for shift_x in range(3):
            pieces = [padded[:, 2 - shift_y:2 - shift_y + count, 2 - shift_x:2 - shift_x + extent_x, 2 - shift_z:2 - shift_z + extent_z, :] for shift_z in range(3)]
            stacked = jnp.concatenate(pieces, axis=-1).reshape(-1, 3 * channels)
            first = shift_y * 9 + shift_x * 3
            kernel = jnp.swapaxes(weight[first:first + 3], 1, 2).reshape(3 * channels, weight.shape[1])
            term = jnp.dot(stacked, kernel, preferred_element_type=jnp.float32)
            total = term if total is None else total + term
    return total.reshape(padded.shape[0], count, extent_x, extent_z, weight.shape[1])


def weight_terms(padded, grad, count):
    extent_x = padded.shape[2] - 2
    extent_z = padded.shape[3] - 2
    channels = padded.shape[4]
    flat_grad = grad.reshape(-1, grad.shape[4])
    blocks = []
    for shift_y in range(3):
        for shift_x in range(3):
            pieces = [padded[:, shift_y:shift_y + count, shift_x:shift_x + extent_x, shift_z:shift_z + extent_z, :] for shift_z in range(3)]
            stacked = jnp.concatenate(pieces, axis=-1).reshape(-1, 3 * channels)
            blocks.append(lax.dot_general(stacked, flat_grad, (((0,), (0,)), ((), ())), preferred_element_type=jnp.float32))
    return jnp.concatenate(blocks, axis=0).reshape(-1)


def fold_taps(hidden):
    batch, rows_here, extent_x, extent_z, channels = hidden.shape
    shaped = hidden.reshape(batch, rows_here // 2, 2, extent_x // 2, 2, extent_z // 2, 2, channels)
    return shaped.transpose(0, 1, 3, 5, 2, 4, 6, 7).reshape(-1, 8 * channels)


def unfold_taps(values, batch, rows_here, extent_x, extent_z, channels):
    shaped = values.reshape(batch, rows_here // 2, extent_x // 2, extent_z // 2, 2, 2, 2, channels)
    return shaped.transpose(0, 1, 4, 2, 5, 3, 6, 7).reshape(batch, rows_here, extent_x, extent_z, channels)


def silu_slope(value):
    sigma = jax.nn.sigmoid(value)
    return sigma * (1.0 + value * (1.0 - sigma))


def reference(features, w_fine, w_down, mixing, cotangent):
    batch, rows_here, extent_x, extent_z, channels = features.shape
    coarse_ch = w_down.shape[2]
    xpadded = jnp.pad(features, ((0, 0), (1, 1), (1, 1), (1, 1), (0, 0)))
    act = forward_conv(xpadded, w_fine, rows_here)
    hidden = (features.astype(jnp.float32) + jax.nn.silu(act)).astype(jnp.bfloat16)
    folded = fold_taps(hidden)
    down_matrix = w_down.reshape(8 * channels, coarse_ch)
    coarse = jnp.dot(folded, down_matrix, preferred_element_type=jnp.float32).astype(jnp.bfloat16)
    coarse = coarse.reshape(batch, rows_here // 2, -1)
    mixed = jnp.stack([jnp.dot(mixing, coarse[item], preferred_element_type=jnp.float32) for item in range(batch)])
    bottleneck = (coarse.astype(jnp.float32) + jax.nn.silu(mixed)).astype(jnp.bfloat16)
    cot = cotangent.astype(jnp.float32)
    mixed_grad = (cot * silu_slope(mixed)).astype(jnp.bfloat16)
    scale = float(batch * rows_here * extent_x * extent_z) ** -0.5
    mixing_grad = None
    spread_list = []
    for item in range(batch):
        term = lax.dot_general(mixed_grad[item], coarse[item], (((1,), (1,)), ((), ())), preferred_element_type=jnp.float32)
        mixing_grad = term if mixing_grad is None else mixing_grad + term
        spread_list.append(lax.dot_general(mixing, mixed_grad[item], (((0,), (0,)), ((), ())), preferred_element_type=jnp.float32))
    mixing_grad = mixing_grad * scale
    coarse_grad = (cot + jnp.stack(spread_list)).astype(jnp.bfloat16)
    flat_coarse = coarse_grad.reshape(-1, coarse_ch)
    down_grad = lax.dot_general(folded, flat_coarse, (((0,), (0,)), ((), ())), preferred_element_type=jnp.float32).reshape(-1) * scale
    hidden_grad = unfold_taps(jnp.dot(flat_coarse, down_matrix.T, preferred_element_type=jnp.float32), batch, rows_here, extent_x, extent_z, channels)
    act_grad = (hidden_grad * silu_slope(act)).astype(jnp.bfloat16)
    gpadded = jnp.pad(act_grad, ((0, 0), (1, 1), (1, 1), (1, 1), (0, 0)))
    feature_grad = (hidden_grad + transposed_conv(gpadded, w_fine, rows_here)).astype(jnp.bfloat16)
    fine_grad = weight_terms(xpadded, act_grad, rows_here) * scale
    return (bottleneck, feature_grad, fine_grad, down_grad, mixing_grad)
```

```python
import functools

import jax
import jax.numpy as jnp
from jax import lax
from jax.experimental import pallas as pl
from jax.experimental.pallas import tpu as pltpu
from jax.sharding import PartitionSpec as P

MESH = pl.DeviceIdType.MESH
F32 = jnp.float32
BF16 = jnp.bfloat16
CONTRACT_LAST = (((1,), (1,)), ((), ()))
CONTRACT_FIRST = (((0,), (0,)), ((), ()))


def fused_body(
    cfg,
    features, w_fine, w_down, mixing, cotangent,
    bottleneck, feature_grad, fine_out, down_out, mixing_out,
    x_halo, g_halo, grad16, pad, x3, g3, xt, act, hid, folded, folded_t,
    stage, fwd_send, fwd_recv, back_send, back_recv, hid_grad,
    fine16, fine_peer, fine_send, fine_recv,
    down16, down_peer, down_send, down_recv,
    mix_send, mix_recv, mix_total, mix_peer,
    fine_half, fine_half_peer, down_half, down_half_peer,
    halo_s, halo_r, fwd_s, fwd_r, back_s, back_r, mix_s, mix_r,
    ghalo_s, ghalo_r, peer_s, peer_r, dpeer_s, dpeer_r,
    fine_s, fine_r, down_s, down_r, last_s, last_r,
):
    n, ex, ez, ch, cc, scale = cfg
    plane = ex * ez
    hx, hz = ex // 2, ez // 2
    lanes = 128
    rows = hx * hz * cc // lanes // n
    halves = cc // lanes
    fine_rows = 27 * ch // n
    part = fine_send.shape[1]
    fine_step = fine_rows - part
    fine_mine = fine_rows // 2
    down_rows = 8 * ch // n
    down_part = down_rows // 2
    me = lax.axis_index("space")
    core = lax.axis_index("sample")
    other = 1 - core

    def to_space(src, dst, send, recv, who):
        return pltpu.make_async_remote_copy(
            src_ref=src, dst_ref=dst, send_sem=send, recv_sem=recv,
            device_id={"space": who}, device_id_type=MESH,
        )

    def to_peer(src, dst, send, recv):
        return pltpu.make_async_remote_copy(
            src_ref=src, dst_ref=dst, send_sem=send, recv_sem=recv,
            device_id={"sample": other}, device_id_type=MESH,
        )

    has_prev, has_next = me > 0, me < n - 1

    @pl.when(me == 0)
    def _():
        x_halo[0] = jnp.zeros(x_halo.shape[1:], BF16)
        g_halo[0] = jnp.zeros(g_halo.shape[1:], BF16)

    @pl.when(me == n - 1)
    def _():
        x_halo[1] = jnp.zeros(x_halo.shape[1:], BF16)
        g_halo[1] = jnp.zeros(g_halo.shape[1:], BF16)

    barrier = pltpu.get_barrier_semaphore()
    for k in range(1, n):
        pl.semaphore_signal(
            barrier, inc=1, device_id={"space": lax.rem(me + k, n)}, device_id_type=MESH
        )
    pl.semaphore_signal(barrier, inc=1, device_id={"sample": other}, device_id_type=MESH)
    pl.semaphore_wait(barrier, n)

    def halo_copies(first, last, halo, send, recv):
        down = to_space(first, halo.at[1], send.at[0], recv.at[1], me - 1)
        up = to_space(last, halo.at[0], send.at[1], recv.at[0], me + 1)
        return down, up

    def start_halo(copies):
        pl.when(has_prev)(copies[0].start)
        pl.when(has_next)(copies[1].start)

    def wait_halo(copies):
        def with_prev():
            copies[0].wait_send()
            copies[1].wait_recv()

        def with_next():
            copies[1].wait_send()
            copies[0].wait_recv()

        pl.when(has_prev)(with_prev)
        pl.when(has_next)(with_next)

    x_copies = halo_copies(features.at[0, 0], features.at[0, 1], x_halo, halo_s, halo_r)
    start_halo(x_copies)

    pad[:, :, 0:8, :] = jnp.zeros((2, ex, 8, ch), F32)
    pad[:, :, 8 + ez : 16 + ez, :] = jnp.zeros((2, ex, 8, ch), F32)
    for rim in (0, ex + 1):
        x3[:, rim] = jnp.zeros((4, ez, 3 * ch), BF16)
        g3[:, rim] = jnp.zeros((4, ez, 3 * ch), BF16)

    def spread_rows(dest, index, row, slot):
        pad[slot, :, 8 : 8 + ez, :] = row.astype(F32)
        dest[index, 1 : 1 + ex, :, 0:ch] = pad[slot, :, 7 : 7 + ez, :].astype(BF16)
        dest[index, 1 : 1 + ex, :, ch : 2 * ch] = row
        dest[index, 1 : 1 + ex, :, 2 * ch : 3 * ch] = pad[slot, :, 9 : 9 + ez, :].astype(BF16)

    def window(source, index, shift):
        return source[index, shift : shift + ex].reshape(plane, 3 * ch)

    def taps(sy, sx):
        first = sy * 9 + sx * 3
        return w_fine[first : first + 3].reshape(3 * ch, ch)

    def mm(a, b):
        return jnp.dot(a, b, preferred_element_type=F32)

    spread_rows(x3, 1, features[0, 0], 0)
    spread_rows(x3, 2, features[0, 1], 1)
    total = None
    for sx in range(3):
        term = mm(window(x3, 1, sx), jnp.concatenate([taps(1, sx), taps(0, sx)], axis=1))
        total = term if total is None else total + term
        total = total + mm(
            window(x3, 2, sx), jnp.concatenate([taps(2, sx), taps(1, sx)], axis=1)
        )
    act[...] = total
    wait_halo(x_copies)
    spread_rows(x3, 0, x_halo[0], 0)
    spread_rows(x3, 3, x_halo[1], 1)
    for side in range(2):
        total = act[:, side * ch : (side + 1) * ch]
        for sx in range(3):
            total = total + mm(window(x3, 3 * side, sx), taps(2 * side, sx))
        act[:, side * ch : (side + 1) * ch] = total
        value = features[0, side].reshape(plane, ch).astype(F32) + total * jax.nn.sigmoid(total)
        hid[side] = value.astype(BF16).astype(F32).reshape(hx, 2, ez, ch)

    for t in range(8):
        i, j, k = t // 4, t // 2 % 2, t % 2
        piece = hid[i, :, j, pl.ds(k, hz, stride=2), :].reshape(hx * hz, ch)
        folded[:, t * ch : (t + 1) * ch] = piece.astype(BF16)
    coarse = mm(folded[...], w_down[...].reshape(8 * ch, cc)).astype(BF16).astype(F32)
    for h in range(halves):
        stage[pl.ds(h, hx * hz, stride=halves), :] = coarse[:, h * lanes : (h + 1) * lanes]
    fwd_send[...] = stage[...].astype(BF16).reshape(n, rows, lanes)

    def exchange(src_of, slots, send, recv):
        out = []
        for k in range(1, n):
            who = lax.rem(me + k, n)
            copy = to_space(src_of(who), slots.at[me], send.at[k - 1], recv.at[k - 1], who)
            copy.start()
            out.append(copy)
        return out

    coarse_copies = exchange(lambda who: fwd_send.at[who], fwd_recv, fwd_s, fwd_r)
    fwd_recv[me] = fwd_send[me]

    folded_t[...] = folded[...].T
    for sx in range(3):
        for j in range(4):
            xt[sx, :, j * plane : (j + 1) * plane] = window(x3, j, sx).T

    for copy in coarse_copies:
        copy.wait()
    stage[...] = fwd_recv[...].reshape(n * rows, lanes).astype(F32)
    columns = jnp.concatenate([stage[pl.ds(r, n, stride=rows), :] for r in range(rows)], axis=1)
    columns16 = columns.astype(BF16)
    mix = mixing[...]
    mixed = mm(mix, columns16)
    sigma = jax.nn.sigmoid(mixed)
    bottleneck[0] = (columns + mixed * sigma).astype(BF16)
    cot = cotangent[0].astype(F32)
    mixed_grad = (cot * (sigma * (1.0 + mixed * (1.0 - sigma)))).astype(BF16)
    spread = lax.dot_general(mix, mixed_grad, CONTRACT_FIRST, preferred_element_type=F32)
    column_grad = cot + spread
    for r in range(rows):
        stage[pl.ds(r, n, stride=rows), :] = column_grad[:, r * lanes : (r + 1) * lanes]
    back_send[...] = stage[...].astype(BF16).reshape(n, rows, lanes)
    back_copies = exchange(lambda who: back_send.at[who], back_recv, back_s, back_r)
    back_recv[me] = back_send[me]
    term = lax.dot_general(mixed_grad, columns16, CONTRACT_LAST, preferred_element_type=F32)
    mix_send[...] = jnp.zeros(mix_send.shape, F32)
    mix_send[:, 0:n] = term
    mix_copies = exchange(lambda who: mix_send, mix_recv, mix_s, mix_r)
    mix_recv[me] = mix_send[...]

    for copy in back_copies:
        copy.wait()
    stage[...] = back_recv[...].reshape(n * rows, lanes).astype(F32)
    flat = jnp.concatenate(
        [stage[pl.ds(h, hx * hz, stride=halves), :] for h in range(halves)], axis=1
    ).astype(BF16)

    for t in range(8):
        i, j, k = t // 4, t // 2 % 2, t % 2
        piece = lax.dot_general(flat, w_down[t], CONTRACT_LAST, preferred_element_type=F32)
        hid_grad[i, :, j, pl.ds(k, hz, stride=2), :] = piece.reshape(hx, hz, ch)
    for side in range(2):
        value = act[:, side * ch : (side + 1) * ch]
        sig = jax.nn.sigmoid(value)
        slope = sig * (1.0 + value * (1.0 - sig))
        grad = hid_grad[side].reshape(plane, ch) * slope
        grad16[side] = grad.astype(BF16).reshape(ex, ez, ch)
    g_copies = halo_copies(grad16.at[0], grad16.at[1], g_halo, ghalo_s, ghalo_r)
    start_halo(g_copies)

    down16[...] = mm(folded_t[...], flat).astype(BF16).reshape(n, down_rows, cc)
    dpeer = to_peer(
        down16.at[:, pl.ds(pl.multiple_of(other * down_part, 16), down_part), :],
        down_peer, dpeer_s, dpeer_r,
    )
    dpeer.start()

    flat_grad = grad16[...].reshape(2 * plane, ch)
    peer_copies = []
    done = 0
    down_copies = []
    for t in range(9):
        sy, sx = t // 3, t % 3
        block = mm(xt[sx, :, sy * plane : (sy + 2) * plane], flat_grad)
        fine16[t * 3 * ch : (t + 1) * 3 * ch, :] = block.astype(BF16)
        while done < n and (done + 1) * fine_rows <= (t + 1) * 3 * ch:
            start = pl.multiple_of(done * fine_rows + other * fine_step, 16)
            copy = to_peer(
                fine16.at[pl.ds(start, part), :], fine_peer.at[done],
                peer_s.at[done], peer_r.at[done],
            )
            copy.start()
            peer_copies.append(copy)
            done += 1
        if t == 3:
            dpeer.wait()
            mine = down16[:, pl.ds(pl.multiple_of(core * down_part, 16), down_part), :]
            down_send[...] = (mine.astype(F32) + down_peer[...].astype(F32)).astype(BF16)
            down_copies = exchange(lambda who: down_send.at[who], down_recv, down_s, down_r)
            down_recv[me] = down_send[me]

    fine_copies = []
    for copy in peer_copies:
        copy.wait()
    for k in range(1, n + 1):
        who = lax.rem(me + k, n)
        start = pl.multiple_of(who * fine_rows + core * fine_step, 16)
        mine = fine16[pl.ds(start, part), :].astype(F32) + fine_peer[who].astype(F32)
        if k < n:
            fine_send[who] = mine.astype(BF16)
            copy = to_space(
                fine_send.at[who], fine_recv.at[me], fine_s.at[k - 1], fine_r.at[k - 1], who
            )
            copy.start()
            fine_copies.append(copy)
        else:
            fine_recv[me] = mine.astype(BF16)

    def turned(i, sx):
        first = i * 9 + sx * 3
        return jnp.concatenate([w_fine[first + 2 - m] for m in range(3)], axis=1)

    def mt(a, b):
        return lax.dot_general(a, b, CONTRACT_LAST, preferred_element_type=F32)

    spread_rows(g3, 1, grad16[0], 0)
    spread_rows(g3, 2, grad16[1], 1)
    total = None
    for sx in range(3):
        term = mt(window(g3, 1, 2 - sx), jnp.concatenate([turned(1, sx), turned(2, sx)], axis=0))
        total = term if total is None else total + term
        total = total + mt(
            window(g3, 2, 2 - sx), jnp.concatenate([turned(0, sx), turned(1, sx)], axis=0)
        )
    act[...] = total
    wait_halo(g_copies)
    spread_rows(g3, 0, g_halo[0], 0)
    spread_rows(g3, 3, g_halo[1], 1)
    for side in range(2):
        total = act[:, side * ch : (side + 1) * ch] + hid_grad[side].reshape(plane, ch)
        for sx in range(3):
            total = total + mt(window(g3, 3 * side, 2 - sx), turned(2 - 2 * side, sx))
        feature_grad[0, side] = total.astype(BF16).reshape(ex, ez, ch)

    for copy in mix_copies:
        copy.wait()
    mix_total[...] = sum(mix_recv[s] for s in range(n)) * scale
    mix_swap = to_peer(mix_total, mix_peer, last_s.at[0], last_r.at[0])
    mix_swap.start()

    for copy in down_copies:
        copy.wait()
    value = sum(down_recv[s].astype(F32) for s in range(n)) * scale
    for h in range(halves):
        down_half[pl.ds(h, down_part, stride=halves), :] = value[:, h * lanes : (h + 1) * lanes]
    down_swap = to_peer(down_half, down_half_peer, last_s.at[1], last_r.at[1])
    down_swap.start()

    for copy in fine_copies:
        copy.wait()
    value = sum(fine_recv[s].astype(F32) for s in range(n)) * scale
    begin = fine_mine - fine_step
    fine_half[...] = jnp.where(core == 0, value[0:fine_mine], value[begin : begin + fine_mine])
    fine_swap = to_peer(fine_half, fine_half_peer, last_s.at[2], last_r.at[2])
    fine_swap.start()

    down_len = down_part * halves
    fine_out[pl.ds(pl.multiple_of(core * fine_mine, 8), fine_mine), :] = fine_half[...]
    down_out[pl.ds(pl.multiple_of(core * down_len, 8), down_len), :] = down_half[...]
    mix_swap.wait()
    mix_total[...] = mix_total[...] + mix_peer[...]
    mixing_out[...] = mix_total[pl.ds(me, 1), 0:n]
    down_swap.wait()
    down_out[pl.ds(pl.multiple_of(other * down_len, 8), down_len), :] = down_half_peer[...]
    fine_swap.wait()
    fine_out[pl.ds(pl.multiple_of(other * fine_mine, 8), fine_mine), :] = fine_half_peer[...]


def fused_fits(mesh, features, w_down):
    n = mesh.shape["space"]
    batch, ny, ex, ez, ch = features.shape
    cc = w_down.shape[2]
    spots = ex * ez // 4
    return (
        batch == mesh.shape["groups"] * mesh.shape["sample"]
        and ny == 2 * n
        and mesh.shape["sample"] == 2
        and n % 8 == 0
        and ch == 128
        and cc % 128 == 0
        and ez % 16 == 0
        and ex % 2 == 0
        and spots % 8 == 0
        and (spots * cc) % (n * 128 * 16) == 0
        and (27 * ch) % (n * 16) == 0
        and (8 * ch) % (n * 32) == 0
    )


def fused(mesh, features, w_fine, w_down, mixing, cotangent):
    n = lax.axis_size("space")
    _, _, ex, ez, ch = features.shape
    cc = w_down.shape[2]
    batch = lax.axis_size("sample")
    scale = float(batch * 2 * n * ex * ez) ** (-0.5)
    plane, spots, lanes = ex * ez, ex * ez // 4, 128
    rows = spots * cc // lanes // n
    fine_rows, down_rows = 27 * ch // n, 8 * ch // n
    half = fine_rows // 2
    part = -(-half // 16) * 16
    down_part = down_rows // 2
    down_len = down_part * cc // lanes
    vm = pltpu.VMEM
    dma = pltpu.SemaphoreType.DMA
    scratch = [
        vm((2, ex, ez, ch), BF16), vm((2, ex, ez, ch), BF16), vm((2, ex, ez, ch), BF16),
        vm((2, ex, ez + 16, ch), F32),
        vm((4, ex + 2, ez, 3 * ch), BF16), vm((4, ex + 2, ez, 3 * ch), BF16),
        vm((3, 3 * ch, 4 * plane), BF16),
        vm((plane, 2 * ch), F32),
        vm((2, ex // 2, 2, ez, ch), F32),
        vm((spots, 8 * ch), BF16), vm((8 * ch, spots), BF16),
        vm((n * rows, lanes), F32),
        vm((n, rows, lanes), BF16), vm((n, rows, lanes), BF16),
        vm((n, rows, lanes), BF16), vm((n, rows, lanes), BF16),
        vm((2, ex // 2, 2, ez, ch), F32),
        vm((27 * ch, ch), BF16),
        vm((n, part, ch), BF16), vm((n, part, ch), BF16), vm((n, part, ch), BF16),
        vm((n, down_rows, cc), BF16),
        vm((n, down_part, cc), BF16), vm((n, down_part, cc), BF16), vm((n, down_part, cc), BF16),
        vm((n, lanes), F32), vm((n, n, lanes), F32), vm((n, lanes), F32), vm((n, lanes), F32),
        vm((half, ch), F32), vm((half, ch), F32),
        vm((down_len, lanes), F32), vm((down_len, lanes), F32),
        dma((2,)), dma((2,)), dma((n - 1,)), dma((n - 1,)), dma((n - 1,)), dma((n - 1,)),
        dma((n - 1,)), dma((n - 1,)),
        dma((2,)), dma((2,)), dma((n,)), dma((n,)), dma, dma,
        dma((n - 1,)), dma((n - 1,)), dma((n - 1,)), dma((n - 1,)), dma((3,)), dma((3,)),
    ]
    spec = pl.BlockSpec(memory_space=pltpu.VMEM)
    shapes = (
        jax.ShapeDtypeStruct(cotangent.shape, BF16),
        jax.ShapeDtypeStruct(features.shape, BF16),
        jax.ShapeDtypeStruct((fine_rows, ch), F32),
        jax.ShapeDtypeStruct((down_rows * cc // lanes, lanes), F32),
        jax.ShapeDtypeStruct((1, n), F32),
    )
    a, b, c, d, e = pl.pallas_call(
        functools.partial(fused_body, (n, ex, ez, ch, cc, scale)),
        out_shape=shapes,
        in_specs=[spec] * 5,
        out_specs=tuple([spec] * 5),
        scratch_shapes=scratch,
        compiler_params=pltpu.CompilerParams(
            collective_id=0, has_side_effects=True, vmem_limit_bytes=50 * 1024 * 1024
        ),
    )(features, w_fine, w_down, mixing, cotangent)
    return a, b, c.reshape(-1), d.reshape(-1), e


def with_halo(array, sides, width):
    for axis, dim in sides:
        devices, length = (lax.axis_size(axis), array.shape[dim])
        up = [(i, (i + 1) % devices) for i in range(devices - 1)]
        down = [(j, i) for i, j in up]
        last = lax.slice_in_dim(array, length - width, length, axis=dim)
        initial = lax.slice_in_dim(array, 0, width, axis=dim)
        before = lax.ppermute(last, axis, up)
        after = lax.ppermute(initial, axis, down)
        array = jnp.concatenate([before, array, after], axis=dim)
    return array


def forward_conv(padded, weight, count):
    extent_x = padded.shape[2] - 2
    extent_z = padded.shape[3] - 2
    channels = padded.shape[4]
    total = None
    for shift_y in range(3):
        for shift_x in range(3):
            pieces = [
                padded[
                    :,
                    shift_y : shift_y + count,
                    shift_x : shift_x + extent_x,
                    shift_z : shift_z + extent_z,
                    :,
                ]
                for shift_z in range(3)
            ]
            stacked = jnp.concatenate(pieces, axis=-1).reshape(-1, 3 * channels)
            first = shift_y * 9 + shift_x * 3
            kernel = weight[first : first + 3].reshape(3 * channels, weight.shape[2])
            term = jnp.dot(stacked, kernel, preferred_element_type=jnp.float32)
            total = term if total is None else total + term
    return total.reshape(padded.shape[0], count, extent_x, extent_z, weight.shape[2])


def transposed_conv(padded, weight, count):
    extent_x = padded.shape[2] - 2
    extent_z = padded.shape[3] - 2
    channels = padded.shape[4]
    total = None
    for shift_y in range(3):
        for shift_x in range(3):
            pieces = [
                padded[
                    :,
                    2 - shift_y : 2 - shift_y + count,
                    2 - shift_x : 2 - shift_x + extent_x,
                    2 - shift_z : 2 - shift_z + extent_z,
                    :,
                ]
                for shift_z in range(3)
            ]
            stacked = jnp.concatenate(pieces, axis=-1).reshape(-1, 3 * channels)
            first = shift_y * 9 + shift_x * 3
            kernel = jnp.swapaxes(weight[first : first + 3], 1, 2).reshape(
                3 * channels, weight.shape[1]
            )
            term = jnp.dot(stacked, kernel, preferred_element_type=jnp.float32)
            total = term if total is None else total + term
    return total.reshape(padded.shape[0], count, extent_x, extent_z, weight.shape[1])


def weight_terms(padded, grad, count):
    extent_x = padded.shape[2] - 2
    extent_z = padded.shape[3] - 2
    channels = padded.shape[4]
    flat_grad = grad.reshape(-1, grad.shape[4])
    blocks = []
    for shift_y in range(3):
        for shift_x in range(3):
            pieces = [
                padded[
                    :,
                    shift_y : shift_y + count,
                    shift_x : shift_x + extent_x,
                    shift_z : shift_z + extent_z,
                    :,
                ]
                for shift_z in range(3)
            ]
            stacked = jnp.concatenate(pieces, axis=-1).reshape(-1, 3 * channels)
            blocks.append(
                lax.dot_general(
                    stacked, flat_grad, (((0,), (0,)), ((), ())), preferred_element_type=jnp.float32
                )
            )
    return jnp.concatenate(blocks, axis=0).reshape(-1)


def fold_taps(hidden):
    batch, rows_here, extent_x, extent_z, channels = hidden.shape
    shaped = hidden.reshape(batch, rows_here // 2, 2, extent_x // 2, 2, extent_z // 2, 2, channels)
    return shaped.transpose(0, 1, 3, 5, 2, 4, 6, 7).reshape(-1, 8 * channels)


def unfold_taps(values, batch, rows_here, extent_x, extent_z, channels):
    shaped = values.reshape(batch, rows_here // 2, extent_x // 2, extent_z // 2, 2, 2, 2, channels)
    return shaped.transpose(0, 1, 4, 2, 5, 3, 6, 7).reshape(
        batch, rows_here, extent_x, extent_z, channels
    )


def silu_slope(value):
    sigma = jax.nn.sigmoid(value)
    return sigma * (1.0 + value * (1.0 - sigma))


def local(features, w_fine, w_down, mixing, cotangent):
    batch, rows_here, extent_x, extent_z, channels = features.shape
    coarse_ch = w_down.shape[2]
    rimmed = with_halo(features, (("space", 1),), 1)
    xpadded = jnp.pad(rimmed, ((0, 0), (0, 0), (1, 1), (1, 1), (0, 0)))
    act = forward_conv(xpadded, w_fine, rows_here)
    hidden = (features.astype(jnp.float32) + jax.nn.silu(act)).astype(jnp.bfloat16)
    folded = fold_taps(hidden)
    down_matrix = w_down.reshape(8 * channels, coarse_ch)
    coarse = jnp.dot(folded, down_matrix, preferred_element_type=jnp.float32).astype(jnp.bfloat16)
    coarse = coarse.reshape(batch, rows_here // 2, -1)
    columns = lax.all_to_all(coarse, "space", split_axis=2, concat_axis=1, tiled=True)
    mixed = jnp.stack([jnp.dot(mixing, columns[0], preferred_element_type=jnp.float32)])
    bottleneck = (columns.astype(jnp.float32) + jax.nn.silu(mixed)).astype(jnp.bfloat16)
    cot = cotangent.astype(jnp.float32)
    mixed_grad = (cot * silu_slope(mixed)).astype(jnp.bfloat16)
    term = lax.dot_general(
        mixed_grad[0], columns[0], (((1,), (1,)), ((), ())), preferred_element_type=jnp.float32
    )
    spread_list = [
        lax.dot_general(
            mixing, mixed_grad[0], (((0,), (0,)), ((), ())), preferred_element_type=jnp.float32
        )
    ]
    column_grad = (cot + jnp.stack(spread_list)).astype(jnp.bfloat16)
    coarse_grad = lax.all_to_all(column_grad, "space", split_axis=1, concat_axis=2, tiled=True)
    flat_coarse = coarse_grad.reshape(-1, coarse_ch)
    down_terms = lax.dot_general(
        folded, flat_coarse, (((0,), (0,)), ((), ())), preferred_element_type=jnp.float32
    ).reshape(-1)
    hidden_grad = unfold_taps(
        jnp.dot(flat_coarse, down_matrix.T, preferred_element_type=jnp.float32),
        batch,
        rows_here,
        extent_x,
        extent_z,
        channels,
    )
    act_grad = (hidden_grad * silu_slope(act)).astype(jnp.bfloat16)
    grad_rim = with_halo(act_grad, (("space", 1),), 1)
    gpadded = jnp.pad(grad_rim, ((0, 0), (0, 0), (1, 1), (1, 1), (0, 0)))
    spread = transposed_conv(gpadded, w_fine, rows_here)
    feature_grad = (hidden_grad + spread).astype(jnp.bfloat16)
    fine_terms = weight_terms(xpadded, act_grad, rows_here)
    scale = float(
        batch * lax.axis_size("sample") * rows_here * lax.axis_size("space") * extent_x * extent_z
    ) ** (-0.5)
    shares = (
        lax.psum_scatter(fine_terms, "space", scatter_dimension=0, tiled=True),
        lax.psum_scatter(down_terms, "space", scatter_dimension=0, tiled=True),
        lax.psum_scatter(term, "space", scatter_dimension=0, tiled=True),
    )
    totals = lax.psum((shares[0], shares[1], shares[2]), "sample")
    return (bottleneck, feature_grad, totals[0] * scale, totals[1] * scale, totals[2] * scale)


def solution(mesh):
    placed = (
        P(("groups", "sample"), "space", None, None, None),
        P(),
        P(),
        P(),
        P(("groups", "sample"), None, "space"),
    )
    out_specs = (
        P(("groups", "sample"), None, "space"),
        P(("groups", "sample"), "space", None, None, None),
        P(("groups", "space")),
        P(("groups", "space")),
        P(("groups", "space"), None),
    )

    def step(features, w_fine, w_down, mixing, cotangent):
        kernel = functools.partial(fused, mesh) if fused_fits(mesh, features, w_down) else local
        mapped = jax.shard_map(
            kernel, mesh=mesh, in_specs=placed, out_specs=out_specs, check_vma=False
        )
        return mapped(features, w_fine, w_down, mixing, cotangent)

    return step
```

```python
import functools

import jax
import jax.numpy as jnp
from jax import lax
from jax.experimental import pallas as pl
from jax.experimental.pallas import tpu as pltpu
from jax.sharding import PartitionSpec as P

MESH = pl.DeviceIdType.MESH
F32 = jnp.float32
BF16 = jnp.bfloat16
CONTRACT_LAST = (((1,), (1,)), ((), ()))
CONTRACT_FIRST = (((0,), (0,)), ((), ()))


def fused_body(
    cfg,
    features_in, w_fine_in, w_down_in, mixing_in, cotangent_in,
    bottleneck, feature_grad, fine_out, down_out, mixing_out,
    features, w_fine, w_down, mixing, cotangent, load_s,
    x_halo, g_halo, grad16, pad, x3, g3, xt, act, hid, folded, folded_t,
    stage, fwd_send, fwd_recv, back_send, back_recv, hid_grad,
    fine16, fine_peer, fine_pair, fine_met, fine_send, fine_recv,
    down16, down_peer, down_pair, down_met, down_send, down_recv,
    mix_send, mix_recv, mix_total, mix_peer,
    fine_half, fine_half_peer, down_half, down_half_peer,
    halo_s, halo_r, fwd_s, fwd_r, back_s, back_r, mix_s, mix_r,
    ghalo_s, ghalo_r, peer_s, peer_r, dpeer_s, dpeer_r,
    pair_s, pair_r, dpair_s, dpair_r, fine_s, fine_r, down_s, down_r, last_s, last_r,
):
    n, ex, ez, ch, cc, scale = cfg
    plane = ex * ez
    hx, hz = ex // 2, ez // 2
    lanes = 128
    rows = hx * hz * cc // lanes // n
    halves = cc // lanes
    fine_rows = 27 * ch // n
    part = fine_send.shape[1]
    fine_step = fine_rows - part
    fine_mine = fine_rows // 2
    down_rows = 8 * ch // n
    down_part = down_rows // 2
    me = lax.axis_index("space")
    core = lax.axis_index("sample")
    other = 1 - core

    def to_space(src, dst, send, recv, who):
        return pltpu.make_async_remote_copy(
            src_ref=src, dst_ref=dst, send_sem=send, recv_sem=recv,
            device_id={"space": who}, device_id_type=MESH,
        )

    def to_peer(src, dst, send, recv):
        return pltpu.make_async_remote_copy(
            src_ref=src, dst_ref=dst, send_sem=send, recv_sem=recv,
            device_id={"sample": other}, device_id_type=MESH,
        )

    has_prev, has_next = me > 0, me < n - 1
    groups = n // 2
    group, side_of = me // 2, lax.rem(me, 2)
    partner = me + 1 - 2 * side_of

    barrier = pltpu.get_barrier_semaphore()
    for k in range(1, n):
        pl.semaphore_signal(
            barrier, inc=1, device_id={"space": lax.rem(me + k, n)}, device_id_type=MESH
        )
    pl.semaphore_signal(barrier, inc=1, device_id={"sample": other}, device_id_type=MESH)
    loads = [
        pltpu.make_async_copy(source, dest, load_s.at[i])
        for i, (source, dest) in enumerate(
            (
                (features_in, features),
                (w_fine_in, w_fine),
                (w_down_in, w_down),
                (mixing_in, mixing),
                (cotangent_in, cotangent),
            )
        )
    ]
    for load in loads:
        load.start()

    @pl.when(me == 0)
    def _():
        x_halo[0] = jnp.zeros(x_halo.shape[1:], BF16)
        g_halo[0] = jnp.zeros(g_halo.shape[1:], BF16)

    @pl.when(me == n - 1)
    def _():
        x_halo[1] = jnp.zeros(x_halo.shape[1:], BF16)
        g_halo[1] = jnp.zeros(g_halo.shape[1:], BF16)

    def halo_copies(first, last, halo, send, recv):
        down = to_space(first, halo.at[1], send.at[0], recv.at[1], me - 1)
        up = to_space(last, halo.at[0], send.at[1], recv.at[0], me + 1)
        return down, up

    def start_halo(copies):
        pl.when(has_prev)(copies[0].start)
        pl.when(has_next)(copies[1].start)

    def wait_halo(copies):
        def with_prev():
            copies[0].wait_send()
            copies[1].wait_recv()

        def with_next():
            copies[1].wait_send()
            copies[0].wait_recv()

        pl.when(has_prev)(with_prev)
        pl.when(has_next)(with_next)

    pad[:, :, 0:8, :] = jnp.zeros((2, ex, 8, ch), F32)
    pad[:, :, 8 + ez : 16 + ez, :] = jnp.zeros((2, ex, 8, ch), F32)
    for rim in (0, ex + 1):
        x3[:, rim] = jnp.zeros((4, ez, 3 * ch), BF16)
        g3[:, rim] = jnp.zeros((4, ez, 3 * ch), BF16)

    def spread_rows(dest, index, row, slot):
        pad[slot, :, 8 : 8 + ez, :] = row.astype(F32)
        dest[index, 1 : 1 + ex, :, 0:ch] = pad[slot, :, 7 : 7 + ez, :].astype(BF16)
        dest[index, 1 : 1 + ex, :, ch : 2 * ch] = row
        dest[index, 1 : 1 + ex, :, 2 * ch : 3 * ch] = pad[slot, :, 9 : 9 + ez, :].astype(BF16)

    def window(source, index, shift):
        return source[index, shift : shift + ex].reshape(plane, 3 * ch)

    def taps(sy, sx):
        first = sy * 9 + sx * 3
        return w_fine[first : first + 3].reshape(3 * ch, ch)

    def mm(a, b):
        return jnp.dot(a, b, preferred_element_type=F32)

    loads[0].wait()
    spread_rows(x3, 1, features[0, 0], 0)
    spread_rows(x3, 2, features[0, 1], 1)
    loads[1].wait()
    total = None
    x_copies = halo_copies(features.at[0, 0], features.at[0, 1], x_halo, halo_s, halo_r)
    for sx in range(3):
        term = mm(window(x3, 1, sx), jnp.concatenate([taps(1, sx), taps(0, sx)], axis=1))
        total = term if total is None else total + term
        total = total + mm(
            window(x3, 2, sx), jnp.concatenate([taps(2, sx), taps(1, sx)], axis=1)
        )
        if sx == 0:
            act[...] = total
            pl.semaphore_wait(barrier, n)
            start_halo(x_copies)
            total = act[...]
    act[...] = total
    wait_halo(x_copies)
    spread_rows(x3, 0, x_halo[0], 0)
    spread_rows(x3, 3, x_halo[1], 1)
    for side in range(2):
        total = act[:, side * ch : (side + 1) * ch]
        for sx in range(3):
            total = total + mm(window(x3, 3 * side, sx), taps(2 * side, sx))
        act[:, side * ch : (side + 1) * ch] = total
        value = features[0, side].reshape(plane, ch).astype(F32) + total * jax.nn.sigmoid(total)
        hid[side] = value.astype(BF16).astype(F32).reshape(hx, 2, ez, ch)

    for t in range(8):
        i, j, k = t // 4, t // 2 % 2, t % 2
        piece = hid[i, :, j, pl.ds(k, hz, stride=2), :].reshape(hx * hz, ch)
        folded[:, t * ch : (t + 1) * ch] = piece.astype(BF16)
    loads[2].wait()
    coarse = mm(folded[...], w_down[...].reshape(8 * ch, cc)).astype(BF16).astype(F32)
    for h in range(halves):
        stage[pl.ds(h, hx * hz, stride=halves), :] = coarse[:, h * lanes : (h + 1) * lanes]
    fwd_send[...] = stage[...].astype(BF16).reshape(n, rows, lanes)

    def exchange(src_of, slots, send, recv):
        out = []
        for k in range(1, n):
            who = lax.rem(me + k, n)
            copy = to_space(src_of(who), slots.at[me], send.at[k - 1], recv.at[k - 1], who)
            copy.start()
            out.append(copy)
        return out

    coarse_copies = exchange(lambda who: fwd_send.at[who], fwd_recv, fwd_s, fwd_r)
    fwd_recv[me] = fwd_send[me]

    loads[3].wait()
    loads[4].wait()
    folded_t[...] = folded[...].T
    for sx in range(3):
        for j in range(4):
            xt[sx, :, j * plane : (j + 1) * plane] = window(x3, j, sx).T

    for copy in coarse_copies:
        copy.wait()
    stage[...] = fwd_recv[...].reshape(n * rows, lanes).astype(F32)
    columns = jnp.concatenate([stage[pl.ds(r, n, stride=rows), :] for r in range(rows)], axis=1)
    columns16 = columns.astype(BF16)
    mix = mixing[...]
    mixed = mm(mix, columns16)
    sigma = jax.nn.sigmoid(mixed)
    bottleneck[0] = (columns + mixed * sigma).astype(BF16)
    cot = cotangent[0].astype(F32)
    mixed_grad = (cot * (sigma * (1.0 + mixed * (1.0 - sigma)))).astype(BF16)
    spread = lax.dot_general(mix, mixed_grad, CONTRACT_FIRST, preferred_element_type=F32)
    column_grad = cot + spread
    for r in range(rows):
        stage[pl.ds(r, n, stride=rows), :] = column_grad[:, r * lanes : (r + 1) * lanes]
    back_send[...] = stage[...].astype(BF16).reshape(n, rows, lanes)
    back_copies = exchange(lambda who: back_send.at[who], back_recv, back_s, back_r)
    back_recv[me] = back_send[me]
    term = lax.dot_general(mixed_grad, columns16, CONTRACT_LAST, preferred_element_type=F32)
    mix_send[...] = jnp.zeros(mix_send.shape, F32)
    mix_send[:, 0:n] = term
    mix_copies = exchange(lambda who: mix_send, mix_recv, mix_s, mix_r)
    mix_recv[me] = mix_send[...]
    value = act[...]
    sig = jax.nn.sigmoid(value)
    act[...] = sig * (1.0 + value * (1.0 - sig))

    for copy in back_copies:
        copy.wait()
    stage[...] = back_recv[...].reshape(n * rows, lanes).astype(F32)
    flat = jnp.concatenate(
        [stage[pl.ds(h, hx * hz, stride=halves), :] for h in range(halves)], axis=1
    ).astype(BF16)

    for t in range(8):
        i, j, k = t // 4, t // 2 % 2, t % 2
        piece = lax.dot_general(flat, w_down[t], CONTRACT_LAST, preferred_element_type=F32)
        hid_grad[i, :, j, pl.ds(k, hz, stride=2), :] = piece.reshape(hx, hz, ch)
    for side in range(2):
        grad = hid_grad[side].reshape(plane, ch) * act[:, side * ch : (side + 1) * ch]
        grad16[side] = grad.astype(BF16).reshape(ex, ez, ch)
    g_copies = halo_copies(grad16.at[0], grad16.at[1], g_halo, ghalo_s, ghalo_r)
    start_halo(g_copies)

    down16[...] = mm(folded_t[...], flat).astype(BF16).reshape(n, down_rows, cc)
    dpeer = to_peer(
        down16.at[:, pl.ds(pl.multiple_of(other * down_part, 16), down_part), :],
        down_peer, dpeer_s, dpeer_r,
    )
    dpeer.start()

    def down_mine(who):
        rows_of = pl.ds(pl.multiple_of(core * down_part, 16), down_part)
        return down16[who, rows_of, :].astype(F32) + down_peer[who].astype(F32)

    def leave(met, outgoing, incoming, send, recv, k, to):
        if k == groups - 1:
            incoming[group] = met
            return []
        outgoing[k] = met
        copy = to_space(
            outgoing.at[k], incoming.at[group], send.at[k], recv.at[k], 2 * to + side_of
        )
        copy.start()
        return [copy]

    flat_grad = grad16[...].reshape(2 * plane, ch)
    peer_copies = []
    done = 0
    down_copies = []
    for t in range(9):
        sy, sx = t // 3, t % 3
        block = mm(xt[sx, :, sy * plane : (sy + 2) * plane], flat_grad)
        fine16[t * 3 * ch : (t + 1) * 3 * ch, :] = block.astype(BF16)
        while done < n and (done + 1) * fine_rows <= (t + 1) * 3 * ch:
            start = pl.multiple_of(done * fine_rows + other * fine_step, 16)
            copy = to_peer(
                fine16.at[pl.ds(start, part), :], fine_peer.at[done],
                peer_s.at[done], peer_r.at[done],
            )
            copy.start()
            peer_copies.append(copy)
            done += 1
        if t == 1:
            dpeer.wait()
            for g in range(groups):
                down_pair[g] = down_mine(2 * g + 1 - side_of).astype(BF16)
            dpair = to_space(down_pair, down_met, dpair_s, dpair_r, partner)
            dpair.start()
        if t == 5:
            dpair.wait()
            for k in range(groups):
                to = lax.rem(group + 1 + k, groups)
                met = (down_mine(2 * to + side_of) + down_met[to].astype(F32)).astype(BF16)
                down_copies += leave(met, down_send, down_recv, down_s, down_r, k, to)

    for copy in peer_copies:
        copy.wait()

    def fine_own(who):
        start = pl.multiple_of(who * fine_rows + core * fine_step, 16)
        return fine16[pl.ds(start, part), :].astype(F32) + fine_peer[who].astype(F32)

    pair_copies = []
    for k in range(groups):
        to = lax.rem(group + 1 + k, groups)
        fine_pair[to] = fine_own(2 * to + 1 - side_of).astype(BF16)
        copy = to_space(fine_pair.at[to], fine_met.at[to], pair_s.at[k], pair_r.at[k], partner)
        copy.start()
        pair_copies.append(copy)

    fine_copies = []

    def pass_on(k):
        to = lax.rem(group + 1 + k, groups)
        pair_copies[k].wait()
        met = (fine_own(2 * to + side_of) + fine_met[to].astype(F32)).astype(BF16)
        fine_copies.extend(leave(met, fine_send, fine_recv, fine_s, fine_r, k, to))

    def turned(i, sx):
        first = i * 9 + sx * 3
        return jnp.concatenate([w_fine[first + 2 - m] for m in range(3)], axis=1)

    def mt(a, b):
        return lax.dot_general(a, b, CONTRACT_LAST, preferred_element_type=F32)

    spread_rows(g3, 1, grad16[0], 0)
    spread_rows(g3, 2, grad16[1], 1)
    total = None
    for sx in range(3):
        term = mt(window(g3, 1, 2 - sx), jnp.concatenate([turned(1, sx), turned(2, sx)], axis=0))
        total = term if total is None else total + term
        total = total + mt(
            window(g3, 2, 2 - sx), jnp.concatenate([turned(0, sx), turned(1, sx)], axis=0)
        )
        if sx == 1:
            act[...] = total
            pass_on(0)
            total = act[...]
    act[...] = total
    for k in range(1, groups - 2):
        pass_on(k)
    wait_halo(g_copies)
    spread_rows(g3, 0, g_halo[0], 0)
    spread_rows(g3, 3, g_halo[1], 1)
    for side in range(2):
        total = act[:, side * ch : (side + 1) * ch] + hid_grad[side].reshape(plane, ch)
        for sx in range(3):
            total = total + mt(window(g3, 3 * side, 2 - sx), turned(2 - 2 * side, sx))
        feature_grad[0, side] = total.astype(BF16).reshape(ex, ez, ch)
        pass_on(groups - 2 + side)

    for copy in mix_copies:
        copy.wait()
    mix_total[...] = sum(mix_recv[s] for s in range(n)) * scale
    mix_swap = to_peer(mix_total, mix_peer, last_s.at[0], last_r.at[0])
    mix_swap.start()

    for copy in down_copies:
        copy.wait()
    value = sum(down_recv[s].astype(F32) for s in range(groups)) * scale
    for h in range(halves):
        down_half[pl.ds(h, down_part, stride=halves), :] = value[:, h * lanes : (h + 1) * lanes]
    down_swap = to_peer(down_half, down_half_peer, last_s.at[1], last_r.at[1])
    down_swap.start()

    for copy in fine_copies:
        copy.wait()
    value = sum(fine_recv[s].astype(F32) for s in range(groups)) * scale
    begin = fine_mine - fine_step
    fine_half[...] = jnp.where(core == 0, value[0:fine_mine], value[begin : begin + fine_mine])
    fine_swap = to_peer(fine_half, fine_half_peer, last_s.at[2], last_r.at[2])
    fine_swap.start()

    down_len = down_part * halves
    fine_out[pl.ds(pl.multiple_of(core * fine_mine, 8), fine_mine), :] = fine_half[...]
    down_out[pl.ds(pl.multiple_of(core * down_len, 8), down_len), :] = down_half[...]
    mix_swap.wait()
    mix_total[...] = mix_total[...] + mix_peer[...]
    mixing_out[...] = mix_total[pl.ds(me, 1), 0:n]
    down_swap.wait()
    down_out[pl.ds(pl.multiple_of(other * down_len, 8), down_len), :] = down_half_peer[...]
    fine_swap.wait()
    fine_out[pl.ds(pl.multiple_of(other * fine_mine, 8), fine_mine), :] = fine_half_peer[...]


def put_out(*refs):
    sources, dests, done = refs[:5], refs[5:10], refs[10]
    copies = [
        pltpu.make_async_copy(source, dest, done.at[i])
        for i, (source, dest) in enumerate(zip(sources, dests))
    ]
    for copy in copies:
        copy.start()
    for copy in copies:
        copy.wait()


def fused_fits(mesh, features, w_down):
    n = mesh.shape["space"]
    batch, ny, ex, ez, ch = features.shape
    cc = w_down.shape[2]
    spots = ex * ez // 4
    return (
        batch == mesh.shape["groups"] * mesh.shape["sample"]
        and ny == 2 * n
        and mesh.shape["sample"] == 2
        and n % 8 == 0
        and ch == 128
        and cc % 128 == 0
        and ez % 16 == 0
        and ex % 2 == 0
        and spots % 8 == 0
        and (spots * cc) % (n * 128 * 16) == 0
        and (27 * ch) % (n * 16) == 0
        and (8 * ch) % (n * 32) == 0
    )


def fused(mesh, features, w_fine, w_down, mixing, cotangent):
    n = lax.axis_size("space")
    _, _, ex, ez, ch = features.shape
    cc = w_down.shape[2]
    batch = lax.axis_size("sample")
    scale = float(batch * 2 * n * ex * ez) ** (-0.5)
    plane, spots, lanes = ex * ez, ex * ez // 4, 128
    rows = spots * cc // lanes // n
    fine_rows, down_rows = 27 * ch // n, 8 * ch // n
    half = fine_rows // 2
    part = -(-half // 16) * 16
    down_part = down_rows // 2
    down_len = down_part * cc // lanes
    vm = pltpu.VMEM
    dma = pltpu.SemaphoreType.DMA
    groups = n // 2
    arrays = (features, w_fine, w_down, mixing, cotangent)
    scratch = [
        *[vm(array.shape, BF16) for array in arrays], dma((5,)),
        vm((2, ex, ez, ch), BF16), vm((2, ex, ez, ch), BF16), vm((2, ex, ez, ch), BF16),
        vm((2, ex, ez + 16, ch), F32),
        vm((4, ex + 2, ez, 3 * ch), BF16), vm((4, ex + 2, ez, 3 * ch), BF16),
        vm((3, 3 * ch, 4 * plane), BF16),
        vm((plane, 2 * ch), F32),
        vm((2, ex // 2, 2, ez, ch), F32),
        vm((spots, 8 * ch), BF16), vm((8 * ch, spots), BF16),
        vm((n * rows, lanes), F32),
        vm((n, rows, lanes), BF16), vm((n, rows, lanes), BF16),
        vm((n, rows, lanes), BF16), vm((n, rows, lanes), BF16),
        vm((2, ex // 2, 2, ez, ch), F32),
        vm((27 * ch, ch), BF16),
        vm((n, part, ch), BF16), *[vm((groups, part, ch), BF16)] * 4,
        vm((n, down_rows, cc), BF16),
        vm((n, down_part, cc), BF16), *[vm((groups, down_part, cc), BF16)] * 4,
        vm((n, lanes), F32), vm((n, n, lanes), F32), vm((n, lanes), F32), vm((n, lanes), F32),
        vm((half, ch), F32), vm((half, ch), F32),
        vm((down_len, lanes), F32), vm((down_len, lanes), F32),
        dma((2,)), dma((2,)), dma((n - 1,)), dma((n - 1,)), dma((n - 1,)), dma((n - 1,)),
        dma((n - 1,)), dma((n - 1,)),
        dma((2,)), dma((2,)), dma((n,)), dma((n,)), dma, dma,
        dma((groups,)), dma((groups,)), dma, dma,
        *[dma((groups - 1,))] * 4, dma((3,)), dma((3,)),
    ]
    spec = pl.BlockSpec(memory_space=pltpu.VMEM)
    far = pl.BlockSpec(memory_space=pltpu.HBM)
    shapes = (
        jax.ShapeDtypeStruct(cotangent.shape, BF16),
        jax.ShapeDtypeStruct(features.shape, BF16),
        jax.ShapeDtypeStruct((fine_rows, ch), F32),
        jax.ShapeDtypeStruct((down_rows * cc // lanes, lanes), F32),
        jax.ShapeDtypeStruct((1, n), F32),
    )
    results = pl.pallas_call(
        functools.partial(fused_body, (n, ex, ez, ch, cc, scale)),
        out_shape=shapes,
        in_specs=[far] * 5,
        out_specs=tuple([spec] * 5),
        scratch_shapes=scratch,
        compiler_params=pltpu.CompilerParams(
            collective_id=0, has_side_effects=True, vmem_limit_bytes=65472 * 1024
        ),
    )(*arrays)
    a, b, c, d, e = pl.pallas_call(
        put_out,
        out_shape=shapes,
        in_specs=[spec] * 5,
        out_specs=tuple([far] * 5),
        scratch_shapes=[dma((5,))],
        compiler_params=pltpu.CompilerParams(vmem_limit_bytes=65472 * 1024),
    )(*results)
    return a, b, c.reshape(-1), d.reshape(-1), e


def with_halo(array, sides, width):
    for axis, dim in sides:
        devices, length = (lax.axis_size(axis), array.shape[dim])
        up = [(i, (i + 1) % devices) for i in range(devices - 1)]
        down = [(j, i) for i, j in up]
        last = lax.slice_in_dim(array, length - width, length, axis=dim)
        initial = lax.slice_in_dim(array, 0, width, axis=dim)
        before = lax.ppermute(last, axis, up)
        after = lax.ppermute(initial, axis, down)
        array = jnp.concatenate([before, array, after], axis=dim)
    return array


def forward_conv(padded, weight, count):
    extent_x = padded.shape[2] - 2
    extent_z = padded.shape[3] - 2
    channels = padded.shape[4]
    total = None
    for shift_y in range(3):
        for shift_x in range(3):
            pieces = [
                padded[
                    :,
                    shift_y : shift_y + count,
                    shift_x : shift_x + extent_x,
                    shift_z : shift_z + extent_z,
                    :,
                ]
                for shift_z in range(3)
            ]
            stacked = jnp.concatenate(pieces, axis=-1).reshape(-1, 3 * channels)
            first = shift_y * 9 + shift_x * 3
            kernel = weight[first : first + 3].reshape(3 * channels, weight.shape[2])
            term = jnp.dot(stacked, kernel, preferred_element_type=jnp.float32)
            total = term if total is None else total + term
    return total.reshape(padded.shape[0], count, extent_x, extent_z, weight.shape[2])


def transposed_conv(padded, weight, count):
    extent_x = padded.shape[2] - 2
    extent_z = padded.shape[3] - 2
    channels = padded.shape[4]
    total = None
    for shift_y in range(3):
        for shift_x in range(3):
            pieces = [
                padded[
                    :,
                    2 - shift_y : 2 - shift_y + count,
                    2 - shift_x : 2 - shift_x + extent_x,
                    2 - shift_z : 2 - shift_z + extent_z,
                    :,
                ]
                for shift_z in range(3)
            ]
            stacked = jnp.concatenate(pieces, axis=-1).reshape(-1, 3 * channels)
            first = shift_y * 9 + shift_x * 3
            kernel = jnp.swapaxes(weight[first : first + 3], 1, 2).reshape(
                3 * channels, weight.shape[1]
            )
            term = jnp.dot(stacked, kernel, preferred_element_type=jnp.float32)
            total = term if total is None else total + term
    return total.reshape(padded.shape[0], count, extent_x, extent_z, weight.shape[1])


def weight_terms(padded, grad, count):
    extent_x = padded.shape[2] - 2
    extent_z = padded.shape[3] - 2
    channels = padded.shape[4]
    flat_grad = grad.reshape(-1, grad.shape[4])
    blocks = []
    for shift_y in range(3):
        for shift_x in range(3):
            pieces = [
                padded[
                    :,
                    shift_y : shift_y + count,
                    shift_x : shift_x + extent_x,
                    shift_z : shift_z + extent_z,
                    :,
                ]
                for shift_z in range(3)
            ]
            stacked = jnp.concatenate(pieces, axis=-1).reshape(-1, 3 * channels)
            blocks.append(
                lax.dot_general(
                    stacked, flat_grad, (((0,), (0,)), ((), ())), preferred_element_type=jnp.float32
                )
            )
    return jnp.concatenate(blocks, axis=0).reshape(-1)


def fold_taps(hidden):
    batch, rows_here, extent_x, extent_z, channels = hidden.shape
    shaped = hidden.reshape(batch, rows_here // 2, 2, extent_x // 2, 2, extent_z // 2, 2, channels)
    return shaped.transpose(0, 1, 3, 5, 2, 4, 6, 7).reshape(-1, 8 * channels)


def unfold_taps(values, batch, rows_here, extent_x, extent_z, channels):
    shaped = values.reshape(batch, rows_here // 2, extent_x // 2, extent_z // 2, 2, 2, 2, channels)
    return shaped.transpose(0, 1, 4, 2, 5, 3, 6, 7).reshape(
        batch, rows_here, extent_x, extent_z, channels
    )


def silu_slope(value):
    sigma = jax.nn.sigmoid(value)
    return sigma * (1.0 + value * (1.0 - sigma))


def local(features, w_fine, w_down, mixing, cotangent):
    batch, rows_here, extent_x, extent_z, channels = features.shape
    coarse_ch = w_down.shape[2]
    rimmed = with_halo(features, (("space", 1),), 1)
    xpadded = jnp.pad(rimmed, ((0, 0), (0, 0), (1, 1), (1, 1), (0, 0)))
    act = forward_conv(xpadded, w_fine, rows_here)
    hidden = (features.astype(jnp.float32) + jax.nn.silu(act)).astype(jnp.bfloat16)
    folded = fold_taps(hidden)
    down_matrix = w_down.reshape(8 * channels, coarse_ch)
    coarse = jnp.dot(folded, down_matrix, preferred_element_type=jnp.float32).astype(jnp.bfloat16)
    coarse = coarse.reshape(batch, rows_here // 2, -1)
    columns = lax.all_to_all(coarse, "space", split_axis=2, concat_axis=1, tiled=True)
    mixed = jnp.stack([jnp.dot(mixing, columns[0], preferred_element_type=jnp.float32)])
    bottleneck = (columns.astype(jnp.float32) + jax.nn.silu(mixed)).astype(jnp.bfloat16)
    cot = cotangent.astype(jnp.float32)
    mixed_grad = (cot * silu_slope(mixed)).astype(jnp.bfloat16)
    term = lax.dot_general(
        mixed_grad[0], columns[0], (((1,), (1,)), ((), ())), preferred_element_type=jnp.float32
    )
    spread_list = [
        lax.dot_general(
            mixing, mixed_grad[0], (((0,), (0,)), ((), ())), preferred_element_type=jnp.float32
        )
    ]
    column_grad = (cot + jnp.stack(spread_list)).astype(jnp.bfloat16)
    coarse_grad = lax.all_to_all(column_grad, "space", split_axis=1, concat_axis=2, tiled=True)
    flat_coarse = coarse_grad.reshape(-1, coarse_ch)
    down_terms = lax.dot_general(
        folded, flat_coarse, (((0,), (0,)), ((), ())), preferred_element_type=jnp.float32
    ).reshape(-1)
    hidden_grad = unfold_taps(
        jnp.dot(flat_coarse, down_matrix.T, preferred_element_type=jnp.float32),
        batch,
        rows_here,
        extent_x,
        extent_z,
        channels,
    )
    act_grad = (hidden_grad * silu_slope(act)).astype(jnp.bfloat16)
    grad_rim = with_halo(act_grad, (("space", 1),), 1)
    gpadded = jnp.pad(grad_rim, ((0, 0), (0, 0), (1, 1), (1, 1), (0, 0)))
    spread = transposed_conv(gpadded, w_fine, rows_here)
    feature_grad = (hidden_grad + spread).astype(jnp.bfloat16)
    fine_terms = weight_terms(xpadded, act_grad, rows_here)
    scale = float(
        batch * lax.axis_size("sample") * rows_here * lax.axis_size("space") * extent_x * extent_z
    ) ** (-0.5)
    shares = (
        lax.psum_scatter(fine_terms, "space", scatter_dimension=0, tiled=True),
        lax.psum_scatter(down_terms, "space", scatter_dimension=0, tiled=True),
        lax.psum_scatter(term, "space", scatter_dimension=0, tiled=True),
    )
    totals = lax.psum((shares[0], shares[1], shares[2]), "sample")
    return (bottleneck, feature_grad, totals[0] * scale, totals[1] * scale, totals[2] * scale)


def solution(mesh):
    placed = (
        P(("groups", "sample"), "space", None, None, None),
        P(),
        P(),
        P(),
        P(("groups", "sample"), None, "space"),
    )
    out_specs = (
        P(("groups", "sample"), None, "space"),
        P(("groups", "sample"), "space", None, None, None),
        P(("groups", "space")),
        P(("groups", "space")),
        P(("groups", "space"), None),
    )

    def step(features, w_fine, w_down, mixing, cotangent):
        kernel = functools.partial(fused, mesh) if fused_fits(mesh, features, w_down) else local
        mapped = jax.shard_map(
            kernel, mesh=mesh, in_specs=placed, out_specs=out_specs, check_vma=False
        )
        return mapped(features, w_fine, w_down, mixing, cotangent)

    return step
```

```python
import functools

import jax
import jax.numpy as jnp
from jax import lax
from jax.experimental import pallas as pl
from jax.experimental.pallas import tpu as pltpu
from jax.sharding import PartitionSpec as P

MESH = pl.DeviceIdType.MESH
F32 = jnp.float32
BF16 = jnp.bfloat16
CONTRACT_LAST = (((1,), (1,)), ((), ()))
CONTRACT_FIRST = (((0,), (0,)), ((), ()))


def fused_body(
    cfg,
    features_in, w_fine_in, w_down_in, mixing_in, cotangent_in,
    bottleneck, feature_grad, fine_out, down_out, mixing_out,
    features, w_fine, w_down, mixing, cotangent, load_s,
    x_halo, g_halo, grad16, pad, x3, g3, xt, act, hid, folded, folded_t,
    stage, fwd_send, fwd_recv, back_send, back_recv, hid_grad,
    fine16, fine_peer, fine_pair, fine_met, fine_send, fine_recv,
    down16, down_peer, down_pair, down_met, down_send, down_recv,
    mix_send, mix_recv, mix_total, mix_peer,
    fine_half, fine_half_peer, down_half, down_half_peer,
    halo_s, halo_r, fwd_s, fwd_r, back_s, back_r, mix_s, mix_r,
    ghalo_s, ghalo_r, peer_s, peer_r, dpeer_s, dpeer_r,
    pair_s, pair_r, dpair_s, dpair_r, fine_s, fine_r, down_s, down_r, last_s, last_r,
):
    n, ex, ez, ch, cc, scale = cfg
    plane = ex * ez
    hx, hz = ex // 2, ez // 2
    lanes = 128
    rows = hx * hz * cc // lanes // n
    halves = cc // lanes
    fine_rows = 27 * ch // n
    part = fine_send.shape[1]
    fine_step = fine_rows - part
    fine_mine = fine_rows // 2
    down_rows = 8 * ch // n
    down_part = down_rows // 2
    me = lax.axis_index("space")
    core = lax.axis_index("sample")
    other = 1 - core

    def to_space(src, dst, send, recv, who):
        return pltpu.make_async_remote_copy(
            src_ref=src, dst_ref=dst, send_sem=send, recv_sem=recv,
            device_id={"space": who}, device_id_type=MESH,
        )

    def to_peer(src, dst, send, recv):
        return pltpu.make_async_remote_copy(
            src_ref=src, dst_ref=dst, send_sem=send, recv_sem=recv,
            device_id={"sample": other}, device_id_type=MESH,
        )

    has_prev, has_next = me > 0, me < n - 1
    groups = n // 2
    group, side_of = me // 2, lax.rem(me, 2)
    partner = me + 1 - 2 * side_of

    barrier = pltpu.get_barrier_semaphore()
    for k in range(1, n):
        pl.semaphore_signal(
            barrier, inc=1, device_id={"space": lax.rem(me + k, n)}, device_id_type=MESH
        )
    pl.semaphore_signal(barrier, inc=1, device_id={"sample": other}, device_id_type=MESH)
    loads = [
        pltpu.make_async_copy(source, dest, load_s.at[i])
        for i, (source, dest) in enumerate(
            (
                (features_in, features),
                (w_fine_in, w_fine),
                (w_down_in, w_down),
                (mixing_in, mixing),
                (cotangent_in, cotangent),
            )
        )
    ]
    for load in loads:
        load.start()

    @pl.when(me == 0)
    def _():
        x_halo[0] = jnp.zeros(x_halo.shape[1:], BF16)
        g_halo[0] = jnp.zeros(g_halo.shape[1:], BF16)

    @pl.when(me == n - 1)
    def _():
        x_halo[1] = jnp.zeros(x_halo.shape[1:], BF16)
        g_halo[1] = jnp.zeros(g_halo.shape[1:], BF16)

    def halo_copies(first, last, halo, send, recv):
        down = to_space(first, halo.at[1], send.at[0], recv.at[1], me - 1)
        up = to_space(last, halo.at[0], send.at[1], recv.at[0], me + 1)
        return down, up

    def start_halo(copies):
        pl.when(has_prev)(copies[0].start)
        pl.when(has_next)(copies[1].start)

    def wait_halo(copies):
        def with_prev():
            copies[0].wait_send()
            copies[1].wait_recv()

        def with_next():
            copies[1].wait_send()
            copies[0].wait_recv()

        pl.when(has_prev)(with_prev)
        pl.when(has_next)(with_next)

    pad[:, :, 0:8, :] = jnp.zeros((2, ex, 8, ch), F32)
    pad[:, :, 8 + ez : 16 + ez, :] = jnp.zeros((2, ex, 8, ch), F32)
    for rim in (0, ex + 1):
        x3[:, rim] = jnp.zeros((4, ez, 3 * ch), BF16)
        g3[:, rim] = jnp.zeros((4, ez, 3 * ch), BF16)

    def spread_rows(dest, index, row, slot):
        pad[slot, :, 8 : 8 + ez, :] = row.astype(F32)
        dest[index, 1 : 1 + ex, :, 0:ch] = pad[slot, :, 7 : 7 + ez, :].astype(BF16)
        dest[index, 1 : 1 + ex, :, ch : 2 * ch] = row
        dest[index, 1 : 1 + ex, :, 2 * ch : 3 * ch] = pad[slot, :, 9 : 9 + ez, :].astype(BF16)

    def window(source, index, shift):
        return source[index, shift : shift + ex].reshape(plane, 3 * ch)

    def taps(sy, sx):
        first = sy * 9 + sx * 3
        return w_fine[first : first + 3].reshape(3 * ch, ch)

    def mm(a, b):
        return jnp.dot(a, b, preferred_element_type=F32)

    loads[0].wait()
    spread_rows(x3, 1, features[0, 0], 0)
    spread_rows(x3, 2, features[0, 1], 1)
    loads[1].wait()
    total = None
    x_copies = halo_copies(features.at[0, 0], features.at[0, 1], x_halo, halo_s, halo_r)
    for sx in range(3):
        term = mm(window(x3, 1, sx), jnp.concatenate([taps(1, sx), taps(0, sx)], axis=1))
        total = term if total is None else total + term
        total = total + mm(
            window(x3, 2, sx), jnp.concatenate([taps(2, sx), taps(1, sx)], axis=1)
        )
        if sx == 0:
            act[...] = total
            pl.semaphore_wait(barrier, n)
            start_halo(x_copies)
            total = act[...]
    act[...] = total
    wait_halo(x_copies)
    spread_rows(x3, 0, x_halo[0], 0)
    spread_rows(x3, 3, x_halo[1], 1)
    for side in range(2):
        total = act[:, side * ch : (side + 1) * ch]
        for sx in range(3):
            total = total + mm(window(x3, 3 * side, sx), taps(2 * side, sx))
        act[:, side * ch : (side + 1) * ch] = total
        value = features[0, side].reshape(plane, ch).astype(F32) + total * jax.nn.sigmoid(total)
        hid[side] = value.astype(BF16).astype(F32).reshape(hx, 2, ez, ch)

    for t in range(8):
        i, j, k = t // 4, t // 2 % 2, t % 2
        piece = hid[i, :, j, pl.ds(k, hz, stride=2), :].reshape(hx * hz, ch)
        folded[:, t * ch : (t + 1) * ch] = piece.astype(BF16)
    loads[2].wait()
    coarse = mm(folded[...], w_down[...].reshape(8 * ch, cc)).astype(BF16).astype(F32)
    for h in range(halves):
        stage[pl.ds(h, hx * hz, stride=halves), :] = coarse[:, h * lanes : (h + 1) * lanes]
    fwd_send[...] = stage[...].astype(BF16).reshape(n, rows, lanes)

    def exchange(src_of, slots, send, recv):
        out = []
        for k in range(1, n):
            who = lax.rem(me + k, n)
            copy = to_space(src_of(who), slots.at[me], send.at[k - 1], recv.at[k - 1], who)
            copy.start()
            out.append(copy)
        return out

    coarse_copies = exchange(lambda who: fwd_send.at[who], fwd_recv, fwd_s, fwd_r)
    fwd_recv[me] = fwd_send[me]

    loads[3].wait()
    loads[4].wait()
    folded_t[...] = folded[...].T
    for sx in range(3):
        for j in range(4):
            xt[sx, :, j * plane : (j + 1) * plane] = window(x3, j, sx).T

    for copy in coarse_copies:
        copy.wait()
    stage[...] = fwd_recv[...].reshape(n * rows, lanes).astype(F32)
    columns = jnp.concatenate([stage[pl.ds(r, n, stride=rows), :] for r in range(rows)], axis=1)
    columns16 = columns.astype(BF16)
    mix = mixing[...]
    mixed = mm(mix, columns16)
    sigma = jax.nn.sigmoid(mixed)
    bottleneck[0] = (columns + mixed * sigma).astype(BF16)
    cot = cotangent[0].astype(F32)
    mixed_grad = (cot * (sigma * (1.0 + mixed * (1.0 - sigma)))).astype(BF16)
    spread = lax.dot_general(mix, mixed_grad, CONTRACT_FIRST, preferred_element_type=F32)
    column_grad = cot + spread
    for r in range(rows):
        stage[pl.ds(r, n, stride=rows), :] = column_grad[:, r * lanes : (r + 1) * lanes]
    back_send[...] = stage[...].astype(BF16).reshape(n, rows, lanes)
    back_copies = exchange(lambda who: back_send.at[who], back_recv, back_s, back_r)
    back_recv[me] = back_send[me]
    term = lax.dot_general(mixed_grad, columns16, CONTRACT_LAST, preferred_element_type=F32)
    mix_send[...] = jnp.zeros(mix_send.shape, F32)
    mix_send[:, 0:n] = term
    mix_copies = exchange(lambda who: mix_send, mix_recv, mix_s, mix_r)
    mix_recv[me] = mix_send[...]
    value = act[...]
    sig = jax.nn.sigmoid(value)
    act[...] = sig * (1.0 + value * (1.0 - sig))

    for copy in back_copies:
        copy.wait()
    stage[...] = back_recv[...].reshape(n * rows, lanes).astype(F32)
    flat = jnp.concatenate(
        [stage[pl.ds(h, hx * hz, stride=halves), :] for h in range(halves)], axis=1
    ).astype(BF16)

    for t in range(8):
        i, j, k = t // 4, t // 2 % 2, t % 2
        piece = lax.dot_general(flat, w_down[t], CONTRACT_LAST, preferred_element_type=F32)
        hid_grad[i, :, j, pl.ds(k, hz, stride=2), :] = piece.reshape(hx, hz, ch)
    for side in range(2):
        grad = hid_grad[side].reshape(plane, ch) * act[:, side * ch : (side + 1) * ch]
        grad16[side] = grad.astype(BF16).reshape(ex, ez, ch)
    g_copies = halo_copies(grad16.at[0], grad16.at[1], g_halo, ghalo_s, ghalo_r)

    down16[...] = mm(folded_t[...], flat).astype(BF16).reshape(n, down_rows, cc)
    dpeer = to_peer(
        down16.at[:, pl.ds(pl.multiple_of(other * down_part, 16), down_part), :],
        down_peer, dpeer_s, dpeer_r,
    )
    dpeer.start()

    def down_mine(who):
        rows_of = pl.ds(pl.multiple_of(core * down_part, 16), down_part)
        return down16[who, rows_of, :].astype(F32) + down_peer[who].astype(F32)

    def leave(met, outgoing, incoming, send, recv, k, to):
        if k == groups - 1:
            incoming[group] = met
            return []
        outgoing[k] = met
        copy = to_space(
            outgoing.at[k], incoming.at[group], send.at[k], recv.at[k], 2 * to + side_of
        )
        copy.start()
        return [copy]

    flat_grad = grad16[...].reshape(2 * plane, ch)
    peer_copies = []
    done = 0
    down_copies = []
    for t in range(9):
        sy, sx = t // 3, t % 3
        block = mm(xt[sx, :, sy * plane : (sy + 2) * plane], flat_grad)
        fine16[t * 3 * ch : (t + 1) * 3 * ch, :] = block.astype(BF16)
        while done < n and (done + 1) * fine_rows <= (t + 1) * 3 * ch:
            start = pl.multiple_of(done * fine_rows + other * fine_step, 16)
            copy = to_peer(
                fine16.at[pl.ds(start, part), :], fine_peer.at[done],
                peer_s.at[done], peer_r.at[done],
            )
            copy.start()
            peer_copies.append(copy)
            done += 1

    dpeer.wait()
    dpair_copies = []
    for k in range(groups):
        to = lax.rem(group + 1 + k, groups)
        down_pair[to] = down_mine(2 * to + 1 - side_of).astype(BF16)
        copy = to_space(down_pair.at[to], down_met.at[to], dpair_s.at[k], dpair_r.at[k], partner)
        copy.start()
        dpair_copies.append(copy)

    for copy in peer_copies:
        copy.wait()

    def fine_own(who):
        start = pl.multiple_of(who * fine_rows + core * fine_step, 16)
        return fine16[pl.ds(start, part), :].astype(F32) + fine_peer[who].astype(F32)

    pair_copies = []
    for k in range(groups):
        to = lax.rem(group + 1 + k, groups)
        fine_pair[to] = fine_own(2 * to + 1 - side_of).astype(BF16)
        copy = to_space(fine_pair.at[to], fine_met.at[to], pair_s.at[k], pair_r.at[k], partner)
        copy.start()
        pair_copies.append(copy)
    start_halo(g_copies)

    for k in range(groups):
        to = lax.rem(group + 1 + k, groups)
        dpair_copies[k].wait()
        met = (down_mine(2 * to + side_of) + down_met[to].astype(F32)).astype(BF16)
        down_copies += leave(met, down_send, down_recv, down_s, down_r, k, to)

    fine_copies = []

    def pass_on(k):
        to = lax.rem(group + 1 + k, groups)
        pair_copies[k].wait()
        met = (fine_own(2 * to + side_of) + fine_met[to].astype(F32)).astype(BF16)
        fine_copies.extend(leave(met, fine_send, fine_recv, fine_s, fine_r, k, to))

    def turned(i, sx):
        first = i * 9 + sx * 3
        return jnp.concatenate([w_fine[first + 2 - m] for m in range(3)], axis=1)

    def mt(a, b):
        return lax.dot_general(a, b, CONTRACT_LAST, preferred_element_type=F32)

    spread_rows(g3, 1, grad16[0], 0)
    spread_rows(g3, 2, grad16[1], 1)
    total = None
    for sx in range(3):
        term = mt(window(g3, 1, 2 - sx), jnp.concatenate([turned(1, sx), turned(2, sx)], axis=0))
        total = term if total is None else total + term
        total = total + mt(
            window(g3, 2, 2 - sx), jnp.concatenate([turned(0, sx), turned(1, sx)], axis=0)
        )
        if sx == 1:
            act[...] = total
            pass_on(0)
            total = act[...]
    act[...] = total
    for k in range(1, groups - 2):
        pass_on(k)
    wait_halo(g_copies)
    spread_rows(g3, 0, g_halo[0], 0)
    spread_rows(g3, 3, g_halo[1], 1)
    for side in range(2):
        total = act[:, side * ch : (side + 1) * ch] + hid_grad[side].reshape(plane, ch)
        for sx in range(3):
            total = total + mt(window(g3, 3 * side, 2 - sx), turned(2 - 2 * side, sx))
        feature_grad[0, side] = total.astype(BF16).reshape(ex, ez, ch)
        pass_on(groups - 2 + side)

    for copy in mix_copies:
        copy.wait()
    mix_total[...] = sum(mix_recv[s] for s in range(n)) * scale
    mix_swap = to_peer(mix_total, mix_peer, last_s.at[0], last_r.at[0])
    mix_swap.start()

    for copy in down_copies:
        copy.wait()
    value = sum(down_recv[s].astype(F32) for s in range(groups)) * scale
    for h in range(halves):
        down_half[pl.ds(h, down_part, stride=halves), :] = value[:, h * lanes : (h + 1) * lanes]
    down_swap = to_peer(down_half, down_half_peer, last_s.at[1], last_r.at[1])
    down_swap.start()

    for copy in fine_copies:
        copy.wait()
    value = sum(fine_recv[s].astype(F32) for s in range(groups)) * scale
    begin = fine_mine - fine_step
    fine_half[...] = jnp.where(core == 0, value[0:fine_mine], value[begin : begin + fine_mine])
    fine_swap = to_peer(fine_half, fine_half_peer, last_s.at[2], last_r.at[2])
    fine_swap.start()

    down_len = down_part * halves
    fine_out[pl.ds(pl.multiple_of(core * fine_mine, 8), fine_mine), :] = fine_half[...]
    down_out[pl.ds(pl.multiple_of(core * down_len, 8), down_len), :] = down_half[...]
    mix_swap.wait()
    mix_total[...] = mix_total[...] + mix_peer[...]
    mixing_out[...] = mix_total[pl.ds(me, 1), 0:n]
    down_swap.wait()
    down_out[pl.ds(pl.multiple_of(other * down_len, 8), down_len), :] = down_half_peer[...]
    fine_swap.wait()
    fine_out[pl.ds(pl.multiple_of(other * fine_mine, 8), fine_mine), :] = fine_half_peer[...]


def put_out(*refs):
    sources, dests, done = refs[:5], refs[5:10], refs[10]
    copies = [
        pltpu.make_async_copy(source, dest, done.at[i])
        for i, (source, dest) in enumerate(zip(sources, dests))
    ]
    for copy in copies:
        copy.start()
    for copy in copies:
        copy.wait()


def fused_fits(mesh, features, w_down):
    n = mesh.shape["space"]
    batch, ny, ex, ez, ch = features.shape
    cc = w_down.shape[2]
    spots = ex * ez // 4
    return (
        batch == mesh.shape["groups"] * mesh.shape["sample"]
        and ny == 2 * n
        and mesh.shape["sample"] == 2
        and n % 8 == 0
        and ch == 128
        and cc % 128 == 0
        and ez % 16 == 0
        and ex % 2 == 0
        and spots % 8 == 0
        and (spots * cc) % (n * 128 * 16) == 0
        and (27 * ch) % (n * 16) == 0
        and (8 * ch) % (n * 32) == 0
    )


def fused(mesh, features, w_fine, w_down, mixing, cotangent):
    n = lax.axis_size("space")
    _, _, ex, ez, ch = features.shape
    cc = w_down.shape[2]
    batch = lax.axis_size("sample")
    scale = float(batch * 2 * n * ex * ez) ** (-0.5)
    plane, spots, lanes = ex * ez, ex * ez // 4, 128
    rows = spots * cc // lanes // n
    fine_rows, down_rows = 27 * ch // n, 8 * ch // n
    half = fine_rows // 2
    part = -(-half // 16) * 16
    down_part = down_rows // 2
    down_len = down_part * cc // lanes
    vm = pltpu.VMEM
    dma = pltpu.SemaphoreType.DMA
    groups = n // 2
    arrays = (features, w_fine, w_down, mixing, cotangent)
    scratch = [
        *[vm(array.shape, BF16) for array in arrays], dma((5,)),
        vm((2, ex, ez, ch), BF16), vm((2, ex, ez, ch), BF16), vm((2, ex, ez, ch), BF16),
        vm((2, ex, ez + 16, ch), F32),
        vm((4, ex + 2, ez, 3 * ch), BF16), vm((4, ex + 2, ez, 3 * ch), BF16),
        vm((3, 3 * ch, 4 * plane), BF16),
        vm((plane, 2 * ch), F32),
        vm((2, ex // 2, 2, ez, ch), F32),
        vm((spots, 8 * ch), BF16), vm((8 * ch, spots), BF16),
        vm((n * rows, lanes), F32),
        vm((n, rows, lanes), BF16), vm((n, rows, lanes), BF16),
        vm((n, rows, lanes), BF16), vm((n, rows, lanes), BF16),
        vm((2, ex // 2, 2, ez, ch), F32),
        vm((27 * ch, ch), BF16),
        vm((n, part, ch), BF16), *[vm((groups, part, ch), BF16)] * 4,
        vm((n, down_rows, cc), BF16),
        vm((n, down_part, cc), BF16), *[vm((groups, down_part, cc), BF16)] * 4,
        vm((n, lanes), F32), vm((n, n, lanes), F32), vm((n, lanes), F32), vm((n, lanes), F32),
        vm((half, ch), F32), vm((half, ch), F32),
        vm((down_len, lanes), F32), vm((down_len, lanes), F32),
        dma((2,)), dma((2,)), dma((n - 1,)), dma((n - 1,)), dma((n - 1,)), dma((n - 1,)),
        dma((n - 1,)), dma((n - 1,)),
        dma((2,)), dma((2,)), dma((n,)), dma((n,)), dma, dma,
        *[dma((groups,))] * 4,
        *[dma((groups - 1,))] * 4, dma((3,)), dma((3,)),
    ]
    spec = pl.BlockSpec(memory_space=pltpu.VMEM)
    far = pl.BlockSpec(memory_space=pltpu.HBM)
    shapes = (
        jax.ShapeDtypeStruct(cotangent.shape, BF16),
        jax.ShapeDtypeStruct(features.shape, BF16),
        jax.ShapeDtypeStruct((fine_rows, ch), F32),
        jax.ShapeDtypeStruct((down_rows * cc // lanes, lanes), F32),
        jax.ShapeDtypeStruct((1, n), F32),
    )
    results = pl.pallas_call(
        functools.partial(fused_body, (n, ex, ez, ch, cc, scale)),
        out_shape=shapes,
        in_specs=[far] * 5,
        out_specs=tuple([spec] * 5),
        scratch_shapes=scratch,
        compiler_params=pltpu.CompilerParams(
            collective_id=0, has_side_effects=True, vmem_limit_bytes=65472 * 1024
        ),
    )(*arrays)
    a, b, c, d, e = pl.pallas_call(
        put_out,
        out_shape=shapes,
        in_specs=[spec] * 5,
        out_specs=tuple([far] * 5),
        scratch_shapes=[dma((5,))],
        compiler_params=pltpu.CompilerParams(vmem_limit_bytes=65472 * 1024),
    )(*results)
    return a, b, c.reshape(-1), d.reshape(-1), e


def with_halo(array, sides, width):
    for axis, dim in sides:
        devices, length = (lax.axis_size(axis), array.shape[dim])
        up = [(i, (i + 1) % devices) for i in range(devices - 1)]
        down = [(j, i) for i, j in up]
        last = lax.slice_in_dim(array, length - width, length, axis=dim)
        initial = lax.slice_in_dim(array, 0, width, axis=dim)
        before = lax.ppermute(last, axis, up)
        after = lax.ppermute(initial, axis, down)
        array = jnp.concatenate([before, array, after], axis=dim)
    return array


def forward_conv(padded, weight, count):
    extent_x = padded.shape[2] - 2
    extent_z = padded.shape[3] - 2
    channels = padded.shape[4]
    total = None
    for shift_y in range(3):
        for shift_x in range(3):
            pieces = [
                padded[
                    :,
                    shift_y : shift_y + count,
                    shift_x : shift_x + extent_x,
                    shift_z : shift_z + extent_z,
                    :,
                ]
                for shift_z in range(3)
            ]
            stacked = jnp.concatenate(pieces, axis=-1).reshape(-1, 3 * channels)
            first = shift_y * 9 + shift_x * 3
            kernel = weight[first : first + 3].reshape(3 * channels, weight.shape[2])
            term = jnp.dot(stacked, kernel, preferred_element_type=jnp.float32)
            total = term if total is None else total + term
    return total.reshape(padded.shape[0], count, extent_x, extent_z, weight.shape[2])


def transposed_conv(padded, weight, count):
    extent_x = padded.shape[2] - 2
    extent_z = padded.shape[3] - 2
    channels = padded.shape[4]
    total = None
    for shift_y in range(3):
        for shift_x in range(3):
            pieces = [
                padded[
                    :,
                    2 - shift_y : 2 - shift_y + count,
                    2 - shift_x : 2 - shift_x + extent_x,
                    2 - shift_z : 2 - shift_z + extent_z,
                    :,
                ]
                for shift_z in range(3)
            ]
            stacked = jnp.concatenate(pieces, axis=-1).reshape(-1, 3 * channels)
            first = shift_y * 9 + shift_x * 3
            kernel = jnp.swapaxes(weight[first : first + 3], 1, 2).reshape(
                3 * channels, weight.shape[1]
            )
            term = jnp.dot(stacked, kernel, preferred_element_type=jnp.float32)
            total = term if total is None else total + term
    return total.reshape(padded.shape[0], count, extent_x, extent_z, weight.shape[1])


def weight_terms(padded, grad, count):
    extent_x = padded.shape[2] - 2
    extent_z = padded.shape[3] - 2
    channels = padded.shape[4]
    flat_grad = grad.reshape(-1, grad.shape[4])
    blocks = []
    for shift_y in range(3):
        for shift_x in range(3):
            pieces = [
                padded[
                    :,
                    shift_y : shift_y + count,
                    shift_x : shift_x + extent_x,
                    shift_z : shift_z + extent_z,
                    :,
                ]
                for shift_z in range(3)
            ]
            stacked = jnp.concatenate(pieces, axis=-1).reshape(-1, 3 * channels)
            blocks.append(
                lax.dot_general(
                    stacked, flat_grad, (((0,), (0,)), ((), ())), preferred_element_type=jnp.float32
                )
            )
    return jnp.concatenate(blocks, axis=0).reshape(-1)


def fold_taps(hidden):
    batch, rows_here, extent_x, extent_z, channels = hidden.shape
    shaped = hidden.reshape(batch, rows_here // 2, 2, extent_x // 2, 2, extent_z // 2, 2, channels)
    return shaped.transpose(0, 1, 3, 5, 2, 4, 6, 7).reshape(-1, 8 * channels)


def unfold_taps(values, batch, rows_here, extent_x, extent_z, channels):
    shaped = values.reshape(batch, rows_here // 2, extent_x // 2, extent_z // 2, 2, 2, 2, channels)
    return shaped.transpose(0, 1, 4, 2, 5, 3, 6, 7).reshape(
        batch, rows_here, extent_x, extent_z, channels
    )


def silu_slope(value):
    sigma = jax.nn.sigmoid(value)
    return sigma * (1.0 + value * (1.0 - sigma))


def local(features, w_fine, w_down, mixing, cotangent):
    batch, rows_here, extent_x, extent_z, channels = features.shape
    coarse_ch = w_down.shape[2]
    rimmed = with_halo(features, (("space", 1),), 1)
    xpadded = jnp.pad(rimmed, ((0, 0), (0, 0), (1, 1), (1, 1), (0, 0)))
    act = forward_conv(xpadded, w_fine, rows_here)
    hidden = (features.astype(jnp.float32) + jax.nn.silu(act)).astype(jnp.bfloat16)
    folded = fold_taps(hidden)
    down_matrix = w_down.reshape(8 * channels, coarse_ch)
    coarse = jnp.dot(folded, down_matrix, preferred_element_type=jnp.float32).astype(jnp.bfloat16)
    coarse = coarse.reshape(batch, rows_here // 2, -1)
    columns = lax.all_to_all(coarse, "space", split_axis=2, concat_axis=1, tiled=True)
    mixed = jnp.stack([jnp.dot(mixing, columns[0], preferred_element_type=jnp.float32)])
    bottleneck = (columns.astype(jnp.float32) + jax.nn.silu(mixed)).astype(jnp.bfloat16)
    cot = cotangent.astype(jnp.float32)
    mixed_grad = (cot * silu_slope(mixed)).astype(jnp.bfloat16)
    term = lax.dot_general(
        mixed_grad[0], columns[0], (((1,), (1,)), ((), ())), preferred_element_type=jnp.float32
    )
    spread_list = [
        lax.dot_general(
            mixing, mixed_grad[0], (((0,), (0,)), ((), ())), preferred_element_type=jnp.float32
        )
    ]
    column_grad = (cot + jnp.stack(spread_list)).astype(jnp.bfloat16)
    coarse_grad = lax.all_to_all(column_grad, "space", split_axis=1, concat_axis=2, tiled=True)
    flat_coarse = coarse_grad.reshape(-1, coarse_ch)
    down_terms = lax.dot_general(
        folded, flat_coarse, (((0,), (0,)), ((), ())), preferred_element_type=jnp.float32
    ).reshape(-1)
    hidden_grad = unfold_taps(
        jnp.dot(flat_coarse, down_matrix.T, preferred_element_type=jnp.float32),
        batch,
        rows_here,
        extent_x,
        extent_z,
        channels,
    )
    act_grad = (hidden_grad * silu_slope(act)).astype(jnp.bfloat16)
    grad_rim = with_halo(act_grad, (("space", 1),), 1)
    gpadded = jnp.pad(grad_rim, ((0, 0), (0, 0), (1, 1), (1, 1), (0, 0)))
    spread = transposed_conv(gpadded, w_fine, rows_here)
    feature_grad = (hidden_grad + spread).astype(jnp.bfloat16)
    fine_terms = weight_terms(xpadded, act_grad, rows_here)
    scale = float(
        batch * lax.axis_size("sample") * rows_here * lax.axis_size("space") * extent_x * extent_z
    ) ** (-0.5)
    shares = (
        lax.psum_scatter(fine_terms, "space", scatter_dimension=0, tiled=True),
        lax.psum_scatter(down_terms, "space", scatter_dimension=0, tiled=True),
        lax.psum_scatter(term, "space", scatter_dimension=0, tiled=True),
    )
    totals = lax.psum((shares[0], shares[1], shares[2]), "sample")
    return (bottleneck, feature_grad, totals[0] * scale, totals[1] * scale, totals[2] * scale)


def solution(mesh):
    placed = (
        P(("groups", "sample"), "space", None, None, None),
        P(),
        P(),
        P(),
        P(("groups", "sample"), None, "space"),
    )
    out_specs = (
        P(("groups", "sample"), None, "space"),
        P(("groups", "sample"), "space", None, None, None),
        P(("groups", "space")),
        P(("groups", "space")),
        P(("groups", "space"), None),
    )

    def step(features, w_fine, w_down, mixing, cotangent):
        kernel = functools.partial(fused, mesh) if fused_fits(mesh, features, w_down) else local
        mapped = jax.shard_map(
            kernel, mesh=mesh, in_specs=placed, out_specs=out_specs, check_vma=False
        )
        return mapped(features, w_fine, w_down, mixing, cotangent)

    return step
```
